32 devices in a mesh: ep: 4 (over z), fsdp: 4 (over y, x), copy: 2 (over core).
Axes of the slice: x: 2, y: 2, z: 4, core: 2. Of those that a mesh axis runs over, the one named last changes fastest.
Arguments:
- master_down: float32 [128, 1408, 2048], P(('copy', 'ep'), None, 'fsdp'), parts along dimension 0, may hold values from -0.21875 to 0.21875
- second_down: bfloat16 [128, 1408, 2048], P(('copy', 'ep'), None, 'fsdp'), parts along dimension 0, may hold values from -0.078125 to 0.078125
- router_weight: float32 [4096, 64], P(('copy', 'fsdp'), 'ep'), parts along dimension 0, may hold values from -0.125 to 0.125
- router_gain: float32 [4096], P(('copy', 'fsdp')), parts along dimension 0, may hold values from 0.25 to 1.75
Outputs:
- final_down: bfloat16 [128, 1408, 2048], P(('copy', 'ep')), parts along dimension 0
- scale_down: float32 [128, 1408], P(('copy', 'ep')), parts along dimension 0
- serve_router: bfloat16 [4096, 64], P('copy'), parts along dimension 0
The draws below stay inside these ranges and needn't reach their ends.
There are 2 independent parts, one for each index of `copy`. The reference program is written for one: setup_inputs(seed, part) draws one part's arguments, and reference() takes and returns one part's arrays. A program takes and returns all parts, laid end to end along the dimension named above; each array names one. Nothing has to cross between parts.
All inputs are finite; a program needn't handle non-finite values. Where the reference program divides by a largest or mean magnitude, that divisor is 1e-20 or more.
Results may differ from the reference program's by a relative error of at most 0.001.
Values may be sent and summed in bfloat16 or wider, within the bound.
A program may use at most 320 MiB of HBM per device.

```python
import jax
import jax.numpy as jnp

EXPERTS = 64
D_MODEL = 2048
D_EXPERT = 1408


def strengthened(values, rng, source, target, parts, factor):
    def block_of(position):
        return (jnp.arange(values.shape[position]) // (values.shape[position] // parts)).reshape((-1,) + (1,) * (values.ndim - 1 - position))

    near = jax.random.permutation(rng, parts)[block_of(target)]
    other_side = (block_of(target) + parts // 2) % parts
    return jnp.where((block_of(source) == near) | (block_of(source) == other_side), factor * values, values)


def block_scale(stream_key, shape, shards, low, high):
    level, own = 1.0, jax.random.fold_in(stream_key, 6)
    for position, shards_of in shards:
        steps = jnp.exp(jax.random.uniform(jax.random.fold_in(own, position), (shards_of,), jnp.float32, low / len(shards), high / len(shards)))
        level = level * jnp.repeat(steps, shape[position] // shards_of).reshape([-1 if axis == position else 1 for axis in range(len(shape))])
    return level


def centred(own_key, extent, scale, most, pieces=(), held_as=jnp.bfloat16):
    drawn = scale * jax.random.normal(own_key, extent, jnp.float32)
    if pieces:
        drawn = drawn * block_scale(own_key, extent, pieces, -0.22, 0.18)
    return jnp.clip(drawn, -most, most).astype(held_as)


def gaussian_with(key, shape, deviation, bound, split, heavy, held_as=jnp.bfloat16):
    result = deviation * jax.random.normal(key, shape, jnp.float32)
    if split:
        result = result * block_scale(key, shape, split, -0.22, 0.18)
    return jnp.clip(strengthened(result, jax.random.fold_in(key, 3), *heavy), -bound, bound).astype(held_as)


def setup_inputs(seed: int = 0, part: int = 0) -> dict:
    keys = jax.random.split(jax.random.key(seed), 5)
    own_keys = jax.random.split(jax.random.fold_in(keys[4], part), 5)
    master_down = gaussian_with(own_keys[0], (EXPERTS, D_EXPERT, D_MODEL), D_EXPERT ** -0.5, 0.21875, ((0, 4), (2, 4)), (2, 1, 4, 2.0), jnp.float32)
    second_down = centred(own_keys[1], (EXPERTS, D_EXPERT, D_MODEL), (D_EXPERT * 4) ** -0.5, 0.078125, ((0, 4), (2, 4)))
    router_weight = centred(own_keys[2], (D_MODEL, EXPERTS), D_MODEL ** -0.5, 0.125, ((0, 4), (1, 4)), jnp.float32)
    router_gain = jnp.clip(1.0 + 0.15 * jax.random.normal(own_keys[3], (D_MODEL,), jnp.float32), 0.25, 1.75)
    return {"master_down": master_down, "second_down": second_down, "router_weight": router_weight, "router_gain": router_gain}


def reference(master_down, second_down, router_weight, router_gain):
    merged_down = master_down + second_down.astype(jnp.float32)
    scale_down = jnp.sum(jnp.abs(merged_down), axis=2) / D_MODEL
    final_down = (merged_down / jnp.expand_dims(scale_down, 2)).astype(jnp.bfloat16)
    serve_router = (router_weight * router_gain[:, None]).astype(jnp.bfloat16)
    return final_down, scale_down, serve_router
```

```python
import jax
import jax.numpy as jnp
from jax import lax
from jax.experimental import pallas as pl
from jax.experimental.pallas import tpu as pltpu
from jax.sharding import PartitionSpec as P


def pieces_of(experts):
    if experts < 8:
        return [experts]
    end = experts // 16 or 1
    return [end, experts - 2 * end, end]


def rows_per_block(rows):
    return max(r for r in range(16, min(rows, 1024) + 1, 16) if rows % r == 0)


def put_first(piece_ref, out_ref):
    out_ref[...] = piece_ref[...]


def put_next(piece_ref, whole_ref, out_ref):
    out_ref[...] = piece_ref[...]


def put(whole, piece, at, experts):
    count, rows, width = piece.shape
    block = rows_per_block(rows)
    spec = pl.BlockSpec((1, block, width), lambda e, r: (e, r, 0))
    first = whole is None
    return pl.pallas_call(
        put_first if first else put_next,
        grid=(count, rows // block),
        in_specs=[spec] if first else [spec, pl.BlockSpec(memory_space=pl.ANY)],
        out_specs=pl.BlockSpec((1, block, width), lambda e, r: (e + at, r, 0)),
        out_shape=jax.ShapeDtypeStruct((experts, rows, width), piece.dtype),
        input_output_aliases={} if first else {1: 0},
        cost_estimate=pl.CostEstimate(flops=0, bytes_accessed=2 * piece.size * piece.dtype.itemsize, transcendentals=0),
        name=f"put_{at}",
    )(*((piece,) if first else (piece, whole)))


def on_device(master_down, second_down, router_weight, router_gain):
    experts, _, width = master_down.shape
    d_model = width * lax.axis_size("fsdp")

    def merged(at, count):
        return master_down[at : at + count] + second_down[at : at + count].astype(jnp.float32)

    def scale(at, count):
        part = jnp.sum(jnp.abs(merged(at, count)), axis=2)
        return jnp.sum(lax.all_gather(part, "fsdp", axis=0), axis=0) / d_model

    def gathered(at, count, scale):
        narrow = (merged(at, count) / scale[:, :, None]).astype(jnp.bfloat16)
        return lax.all_gather(narrow, "fsdp", axis=2, tiled=True)

    pieces = pieces_of(experts)
    first = pieces[0]
    scales = [scale(0, first)]
    if experts > first:
        scales.append(scale(first, experts - first))
    scale_down = jnp.concatenate(scales, axis=0)

    blocks, at = [], 0
    for number, count in enumerate(pieces):
        own = scales[0] if number == 0 else scales[1][at - first : at - first + count]
        blocks.append((at, gathered(at, count, own)))
        at += count

    part_router = (router_weight * router_gain[:, None]).astype(jnp.bfloat16)
    row_router = lax.all_gather(part_router, "fsdp", axis=0, tiled=True)
    serve_router = lax.all_gather(row_router, "ep", axis=1, tiled=True)

    final_down = None
    for at, block in blocks:
        final_down = put(final_down, block, at, experts)
    return (final_down, scale_down, serve_router)


def solution(mesh):
    return jax.shard_map(
        on_device,
        mesh=mesh,
        in_specs=(
            P(("copy", "ep"), None, "fsdp"),
            P(("copy", "ep"), None, "fsdp"),
            P(("copy", "fsdp"), "ep"),
            P(("copy", "fsdp")),
        ),
        out_specs=(P(("copy", "ep"), None, None), P(("copy", "ep"), None), P("copy", None)),
        check_vma=False,
    )
```
